32 devices in a mesh: grp: 4 (over y, x), col: 8 (over z, core).
Axes of the slice: x: 2, y: 2, z: 4, core: 2. Of those that a mesh axis runs over, the one named last changes fastest.
Arguments:
- right_side: float32 [2048, 2048], P('grp', 'col'), may hold values from -6 to 6
- solved_factor: float32 [2048, 6144], P('grp', 'col'), may hold values from -0.078125 to 0.078125
- solved_users: float32 [6144, 2048], P('col'), may hold values from -6 to 6
- diag_inverse: float32 [2048, 512], P('grp'), may hold values from -0.25 to 0.25
- coupling: float32 [2048, 1536], P('grp'), may hold values from -0.25 to 0.25
Outputs:
- solution: float32 [2048, 2048], P('grp', 'col')
The draws below stay inside these ranges and needn't reach their ends.
All inputs are finite; a program needn't handle non-finite values.
Results may differ from the reference program's by a relative error of at most 0.0001.
Values sent between devices are 32-bit elements; how exact they have to be, the bound alone decides.
A program may use at most 64 MiB of HBM per device.

```python
import jax
import jax.numpy as jnp
from jax import lax

ITEMS = 2048
BLOCK = 512
SOLVED = 6144
WINDOW = 2048
N_GRP = 4


def with_spikes(entries, rng, source, target, parts, factor):
    owner, partner = [(jnp.arange(entries.shape[axis_at]) // (entries.shape[axis_at] // parts)).reshape([-1 if axis == axis_at else 1 for axis in range(entries.ndim)]) for axis_at in (source, target)]
    chosen = jax.random.permutation(rng, parts)[partner]
    strong = (owner == chosen) | (owner == (partner + parts // 2) % parts)
    return jnp.where(strong, factor * entries, entries)


def levels(own_key, dims, cuts, low, high):
    level = 1.0
    for axis_at, parts in cuts:
        heights = jax.random.uniform(jax.random.fold_in(jax.random.fold_in(own_key, 6), axis_at), (parts,), jnp.float32, low / len(cuts), high / len(cuts))
        level = level * jnp.repeat(jnp.exp(heights), dims[axis_at] // parts).reshape((-1,) + (1,) * (len(dims) - 1 - axis_at))
    return level


def normal_values(rng, shape, width, reach, split=(), kind=jnp.bfloat16):
    values = jax.random.normal(rng, shape, jnp.float32) * width
    if len(split) > 0:
        values = levels(rng, shape, split, -0.22, 0.18) * values
    return jnp.clip(values, min=-reach, max=reach).astype(kind)


def noise_with(stream_key, extent, scale, reach, cuts, heavy, kind=jnp.bfloat16):
    entries = scale * jax.random.normal(stream_key, extent, jnp.float32)
    if cuts:
        entries = entries * levels(stream_key, extent, cuts, -0.22, 0.18)
    return jnp.clip(with_spikes(entries, jax.random.fold_in(stream_key, 3), *heavy), -reach, reach).astype(kind)


def setup_inputs(seed: int = 0) -> dict:
    arg_keys = jax.random.split(jax.random.key(seed), 6)
    return {
        "right_side": normal_values(arg_keys[0], (WINDOW, ITEMS), 1.0, 6.0, ((0, 4), (1, 8)), jnp.float32),
        "solved_factor": normal_values(arg_keys[1], (WINDOW, SOLVED), SOLVED ** -0.5, 0.078125, ((0, 4), (1, 8)), jnp.float32),
        "solved_users": noise_with(arg_keys[2], (SOLVED, ITEMS), 1.0, 6.0, ((0, 8),), (0, 1, 8, 2.0), jnp.float32),
        "diag_inverse": normal_values(arg_keys[3], (WINDOW, BLOCK), BLOCK ** -0.5, 0.25, ((0, 4),), jnp.float32),
        "coupling": normal_values(arg_keys[4], (WINDOW, BLOCK * (N_GRP - 1)), BLOCK ** -0.5, 0.25, ((0, 4),), jnp.float32),
    }


highest = lax.Precision.HIGHEST


def product(left, right):
    return jnp.dot(left, right, precision=highest, preferred_element_type=jnp.float32)


def reference(right_side, solved_factor, solved_users, diag_inverse, coupling):
    reduced = right_side - product(solved_factor, solved_users)
    solved_blocks = []
    for group in range(N_GRP):
        rows = slice(group * BLOCK, (group + 1) * BLOCK)
        residue = reduced[rows]
        for earlier in range(group):
            coupling_block = coupling[rows, earlier * BLOCK:(earlier + 1) * BLOCK]
            residue = residue - product(coupling_block, solved_blocks[earlier])
        solved_blocks.append(product(diag_inverse[rows], residue))
    return jnp.concatenate(solved_blocks, axis=0)
```

```python
import functools

import jax
import jax.numpy as jnp
from jax import lax
from jax.experimental import pallas as pl
from jax.experimental.pallas import tpu as pltpu
from jax.sharding import PartitionSpec as P

highest = lax.Precision.HIGHEST
MESH = pl.DeviceIdType.MESH
LANES = 128


def broadcast(block, axis, source):
    block = jnp.where(lax.axis_index(axis) == source, block, jnp.zeros_like(block))
    return lax.psum(block, axis)


def apply_plain(matrix, vector):
    return jnp.dot(matrix, vector, precision=highest, preferred_element_type=jnp.float32)


def run_chain(residue, diag_inverse, coupling, apply_left):
    groups = lax.axis_size("grp")
    position = lax.axis_index("grp")
    block_rows = diag_inverse.shape[0]
    result = jnp.zeros_like(residue)
    for section_index in range(groups):
        candidate = apply_left(diag_inverse, residue)
        result = jnp.where(position == section_index, candidate, result)
        if section_index + 1 < groups:
            solved = broadcast(candidate, "grp", section_index)
            coupling_block = coupling[
                :, section_index * block_rows : (section_index + 1) * block_rows
            ]
            residue = jnp.where(
                position > section_index, residue - apply_left(coupling_block, solved), residue
            )
    return result


def by_collectives(right_side, solved_factor, solved_users, diag_inverse, coupling):
    partials = jnp.dot(
        solved_factor, solved_users, precision=highest, preferred_element_type=jnp.float32
    )
    shares = lax.psum_scatter(partials, "col", scatter_dimension=1, tiled=True)
    residue = right_side - shares
    return run_chain(residue, diag_inverse, coupling, apply_plain)


def halves(x):
    high = x.astype(jnp.bfloat16)
    return high, (x - high.astype(jnp.float32)).astype(jnp.bfloat16)


def left_form(x):
    high, low = halves(x)
    return jnp.concatenate([high, high, low], axis=1)


def right_form(x):
    high, low = halves(x)
    return jnp.concatenate([high, low, high], axis=0)


def dot(a, b):
    return jnp.dot(a, b, preferred_element_type=jnp.float32)


def kernel(
    groups, chips, pieces,
    rhs_hbm, factor_hbm, users_hbm, diag_hbm, coupling_hbm,
    out_ref,
    rhs, factor, users, diag, coupling,
    factor3, diag3, effect3,
    own, give, take, from_low, from_high, total, spare, solved, arrived,
    load_sem, users_sem, give_sem, take_sem, hop_sem, low_sem, high_sem,
    spare_sem, total_sem, solved_sem, arrived_sem,
):
    g = lax.axis_index("grp")
    c = lax.axis_index("col")
    z = c // 2
    e = c % 2
    rows = rhs.shape[0]
    half = rows // 2
    width = rhs.shape[1]
    partner = (g, z * 2 + (1 - e))
    above = (g, c + 2)
    below = (g, c - 2)

    def block_of(b):
        j = b % chips
        return (b // chips) * chips + jnp.where(2 * z < chips, chips - 1 - j, j)

    loads = []
    for part in range(2):
        source = pl.multiple_of((e if part == 0 else 1 - e) * half, half)
        loads.append(pltpu.make_async_copy(
            factor_hbm.at[pl.ds(source, half)], factor.at[pl.ds(part * half, half)],
            load_sem.at[part]))
    later = [
        pltpu.make_async_copy(diag_hbm, diag, load_sem.at[2]),
        pltpu.make_async_copy(coupling_hbm, coupling, load_sem.at[3]),
        pltpu.make_async_copy(rhs_hbm, rhs, load_sem.at[4]),
    ]

    def users_load(b):
        i = block_of(b)
        column = pl.multiple_of(((i % chips) * 2 + i // chips) * width, width)
        return pltpu.make_async_copy(
            users_hbm.at[:, pl.ds(column, width)], users.at[b], users_sem.at[b])

    for copy in loads:
        copy.start()

    @pl.loop(0, 2 * chips)
    def _(b):
        users_load(b).start()

    for copy in later:
        copy.start()

    barrier = pltpu.get_barrier_semaphore()
    pl.semaphore_signal(barrier, inc=1, device_id=partner, device_id_type=MESH)
    for step in range(1, groups):
        pl.semaphore_signal(
            barrier, inc=1, device_id=((g + step) % groups, c), device_id_type=MESH)

    @pl.when(z > 0)
    def _():
        pl.semaphore_signal(barrier, inc=1, device_id=below, device_id_type=MESH)

    @pl.when(z < chips - 1)
    def _():
        pl.semaphore_signal(barrier, inc=1, device_id=above, device_id_type=MESH)

    pl.semaphore_wait(
        barrier, groups + jnp.where(z > 0, 1, 0) + jnp.where(z < chips - 1, 1, 0))

    for copy in loads:
        copy.wait()
    factor3[...] = left_form(factor[...])

    def give_copy(i):
        return pltpu.make_async_remote_copy(
            src_ref=give.at[i], dst_ref=take.at[i], send_sem=give_sem.at[i],
            recv_sem=take_sem.at[i], device_id=partner, device_id_type=MESH)

    def up(i, q):
        return pltpu.make_async_remote_copy(
            src_ref=own.at[i, q], dst_ref=from_low.at[i, q], send_sem=hop_sem.at[i, q],
            recv_sem=low_sem.at[i, q], device_id=above, device_id_type=MESH)

    def down(i, q):
        return pltpu.make_async_remote_copy(
            src_ref=own.at[i, q], dst_ref=from_high.at[i, q], send_sem=hop_sem.at[i, q],
            recv_sem=high_sem.at[i, q], device_id=below, device_id_type=MESH)

    def send_first(i, q):
        d = i % chips

        @pl.when(jnp.logical_and(z == 0, d > 0))
        def _():
            up(i, q).start()

        if chips > 1:
            @pl.when(jnp.logical_and(z == chips - 1, d < chips - 1))
            def _():
                down(i, q).start()

    def merge(b):
        i = block_of(b)
        give_copy(i).wait()
        own[i] = own[i] + take[i]
        send_first(i, 0)

    @pl.loop(0, 2 * chips)
    def _(b):
        users_load(b).wait()
        i = block_of(b)
        product = dot(factor3[...], right_form(users[b]))
        for q in range(pieces):
            columns = slice(q * LANES, (q + 1) * LANES)
            own[i, q] = product[:half, columns]
            give[i, q] = product[half:, columns]
        give_copy(i).start()

        @pl.when(b > 0)
        def _():
            merge(b - 1)

    merge(2 * chips - 1)
    for q in range(1, pieces):
        @pl.loop(0, 2 * chips)
        def _(b):
            send_first(block_of(b), q)

    for copy in later:
        copy.wait()
    diag3[...] = left_form(diag[...])
    for h in range(groups - 1):
        @pl.loop(0, rows // (2 * LANES))
        def _(n):
            columns = pl.multiple_of(n * 2 * LANES, 2 * LANES)
            product = dot(
                diag3[...], right_form(coupling[:, pl.ds(h * rows + columns, 2 * LANES)]))
            high, low = halves(product)
            effect3[h, :, pl.ds(columns, 2 * LANES)] = high
            effect3[h, :, pl.ds(rows + columns, 2 * LANES)] = high
            effect3[h, :, pl.ds(2 * rows + columns, 2 * LANES)] = low

    def total_copy(side, q):
        start = pl.multiple_of(e * half, half)
        return pltpu.make_async_remote_copy(
            src_ref=spare.at[q], dst_ref=total.at[q, pl.ds(start, half)],
            send_sem=spare_sem.at[q], recv_sem=total_sem.at[q],
            device_id=partner, device_id_type=MESH)

    def reduce_piece(p):
        q = p // 2
        side = p % 2
        for s in range(chips - 1):
            right = side * chips + chips - 1 - s
            left = side * chips + s

            @pl.when(jnp.logical_and(z > 0, chips - 1 - s > z))
            def _():
                up(right, q).wait_recv()
                own[right, q] = own[right, q] + from_low[right, q]
                up(right, q).start()

            @pl.when(jnp.logical_and(z < chips - 1, s < z))
            def _():
                down(left, q).wait_recv()
                own[left, q] = own[left, q] + from_high[left, q]
                down(left, q).start()

        mine = side * chips + z

        @pl.when(z > 0)
        def _():
            up(mine, q).wait_recv()
            own[mine, q] = own[mine, q] + from_low[mine, q]

        @pl.when(z < chips - 1)
        def _():
            down(mine, q).wait_recv()
            own[mine, q] = own[mine, q] + from_high[mine, q]

        @pl.when(side == e)
        def _():
            total[q, pl.ds(pl.multiple_of(e * half, half), half)] = own[mine, q]

        @pl.when(side != e)
        def _():
            spare[q] = own[mine, q]
            total_copy(side, q).start()

    def solved_copy(source, target, q):
        return pltpu.make_async_remote_copy(
            src_ref=solved.at[q], dst_ref=arrived.at[source, q],
            send_sem=solved_sem.at[target, q], recv_sem=arrived_sem.at[source, q],
            device_id=(target, c), device_id_type=MESH)

    def solve_piece(q):
        columns = pl.ds(pl.multiple_of(q * LANES, LANES), LANES)
        total_copy(e, q).wait_recv()
        solved[q] = dot(diag3[...], right_form(rhs[:, columns] - total[q]))
        for h in range(groups - 1):
            @pl.when(h < g)
            def _():
                solved_copy(h, 0, q).wait_recv()
                solved[q] = solved[q] - dot(effect3[h], right_form(arrived[h, q]))
        for target in range(1, groups):
            @pl.when(target > g)
            def _():
                solved_copy(g, target, q).start()
        out_ref[:, columns] = solved[q]

    count = 2 * pieces

    @pl.loop(0, count + groups - 1)
    def _(t):
        @pl.when(t < count)
        def _():
            reduce_piece(t)

        p = t - g

        @pl.when(jnp.logical_and(jnp.logical_and(p >= 0, p < count), (p + 2 * groups) % 2 == e))
        def _():
            solve_piece(p // 2)

    @pl.loop(0, 2 * chips)
    def _(i):
        @pl.when(i % chips != z)
        def _():
            for q in range(pieces):
                pltpu.make_async_remote_copy(
                    src_ref=own.at[i, q], dst_ref=from_low.at[i, q], send_sem=hop_sem.at[i, q],
                    recv_sem=low_sem.at[i, q], device_id=partner, device_id_type=MESH
                ).wait_send()

    for q in range(pieces):
        total_copy(0, q).wait_send()
        for target in range(1, groups):
            @pl.when(target > g)
            def _():
                solved_copy(g, target, q).wait_send()


def by_kernel(right_side, solved_factor, solved_users, diag_inverse, coupling):
    groups = lax.axis_size("grp")
    chips = lax.axis_size("col") // 2
    rows, width = right_side.shape
    depth = solved_factor.shape[1]
    half = rows // 2
    pieces = width // LANES
    f32, bf16 = jnp.float32, jnp.bfloat16
    unit = (half, LANES)
    blocks = 2 * chips
    dma = pltpu.SemaphoreType.DMA
    scratch = [
        pltpu.VMEM((rows, width), f32),
        pltpu.VMEM((rows, depth), f32),
        pltpu.VMEM((blocks, depth, width), f32),
        pltpu.VMEM((rows, rows), f32),
        pltpu.VMEM(coupling.shape, f32),
        pltpu.VMEM((rows, 3 * depth), bf16),
        pltpu.VMEM((rows, 3 * rows), bf16),
        pltpu.VMEM((groups - 1, rows, 3 * rows), bf16),
        pltpu.VMEM((blocks, pieces) + unit, f32),
        pltpu.VMEM((blocks, pieces) + unit, f32),
        pltpu.VMEM((blocks, pieces) + unit, f32),
        pltpu.VMEM((blocks, pieces) + unit, f32),
        pltpu.VMEM((blocks, pieces) + unit, f32),
        pltpu.VMEM((pieces, rows, LANES), f32),
        pltpu.VMEM((pieces,) + unit, f32),
        pltpu.VMEM((pieces, rows, LANES), f32),
        pltpu.VMEM((groups - 1, pieces, rows, LANES), f32),
        dma((5,)), dma((blocks,)), dma((blocks,)), dma((blocks,)),
        dma((blocks, pieces)), dma((blocks, pieces)), dma((blocks, pieces)),
        dma((pieces,)), dma((pieces,)), dma((groups, pieces)), dma((groups, pieces)),
    ]
    return pl.pallas_call(
        functools.partial(kernel, groups, chips, pieces),
        out_shape=jax.ShapeDtypeStruct((rows, width), f32),
        in_specs=[pl.BlockSpec(memory_space=pl.ANY)] * 5,
        out_specs=pl.BlockSpec(memory_space=pltpu.VMEM),
        scratch_shapes=scratch,
        compiler_params=pltpu.CompilerParams(
            collective_id=0, has_side_effects=True, vmem_limit_bytes=60 << 20),
    )(right_side, solved_factor, solved_users, diag_inverse, coupling)


def on_device(right_side, *others):
    whole_tiles = right_side.shape[1] % LANES == 0 and lax.axis_size("col") % 2 == 0
    return (by_kernel if whole_tiles else by_collectives)(right_side, *others)


def solution(mesh):
    placed = (P("grp", "col"), P("grp", "col"), P("col", None), P("grp", None), P("grp", None))
    return jax.shard_map(
        on_device, mesh=mesh, in_specs=placed, out_specs=P("grp", "col"), check_vma=False
    )
```

```python
import functools

import jax
import jax.numpy as jnp
from jax import lax
from jax.experimental import pallas as pl
from jax.experimental.pallas import tpu as pltpu
from jax.sharding import PartitionSpec as P

highest = lax.Precision.HIGHEST
MESH = pl.DeviceIdType.MESH
LANES = 128


def broadcast(block, axis, source):
    block = jnp.where(lax.axis_index(axis) == source, block, jnp.zeros_like(block))
    return lax.psum(block, axis)


def apply_plain(matrix, vector):
    return jnp.dot(matrix, vector, precision=highest, preferred_element_type=jnp.float32)


def run_chain(residue, diag_inverse, coupling, apply_left):
    groups = lax.axis_size("grp")
    position = lax.axis_index("grp")
    block_rows = diag_inverse.shape[0]
    result = jnp.zeros_like(residue)
    for section_index in range(groups):
        candidate = apply_left(diag_inverse, residue)
        result = jnp.where(position == section_index, candidate, result)
        if section_index + 1 < groups:
            solved = broadcast(candidate, "grp", section_index)
            coupling_block = coupling[
                :, section_index * block_rows : (section_index + 1) * block_rows
            ]
            residue = jnp.where(
                position > section_index, residue - apply_left(coupling_block, solved), residue
            )
    return result


def by_collectives(right_side, solved_factor, solved_users, diag_inverse, coupling):
    partials = jnp.dot(
        solved_factor, solved_users, precision=highest, preferred_element_type=jnp.float32
    )
    shares = lax.psum_scatter(partials, "col", scatter_dimension=1, tiled=True)
    residue = right_side - shares
    return run_chain(residue, diag_inverse, coupling, apply_plain)


def halves(x):
    high = x.astype(jnp.bfloat16)
    return high, (x - high.astype(jnp.float32)).astype(jnp.bfloat16)


def left_form(x):
    high, low = halves(x)
    return jnp.concatenate([high, high, low], axis=1)


def right_form(x):
    high, low = halves(x)
    return jnp.concatenate([high, low, high], axis=0)


def dot(a, b):
    return jnp.dot(a, b, preferred_element_type=jnp.float32)


def kernel(
    groups, chips, pieces,
    rhs_hbm, factor_hbm, users_hbm, diag_hbm, coupling_hbm,
    out_ref,
    rhs, factor, users, diag, coupling,
    factor3, diag3, effect3,
    own, give, take, from_low, from_high, total, spare, solved, arrived,
    load_sem, users_sem, give_sem, take_sem, hop_sem, low_sem, high_sem,
    spare_sem, total_sem, solved_sem, arrived_sem,
):
    g = lax.axis_index("grp")
    c = lax.axis_index("col")
    z = c // 2
    e = c % 2
    rows = rhs.shape[0]
    half = rows // 2
    width = rhs.shape[1]
    partner = (g, z * 2 + (1 - e))
    above = (g, c + 2)
    below = (g, c - 2)

    def block_of(b):
        j = b % chips
        return (b // chips) * chips + jnp.where(2 * z < chips, chips - 1 - j, j)

    loads = []
    for part in range(2):
        source = pl.multiple_of((e if part == 0 else 1 - e) * half, half)
        loads.append(pltpu.make_async_copy(
            factor_hbm.at[pl.ds(source, half)], factor.at[pl.ds(part * half, half)],
            load_sem.at[part]))
    later = [
        pltpu.make_async_copy(diag_hbm, diag, load_sem.at[2]),
        pltpu.make_async_copy(coupling_hbm, coupling, load_sem.at[3]),
        pltpu.make_async_copy(rhs_hbm, rhs, load_sem.at[4]),
    ]

    def users_load(b):
        i = block_of(b)
        column = pl.multiple_of(((i % chips) * 2 + i // chips) * width, width)
        return pltpu.make_async_copy(
            users_hbm.at[:, pl.ds(column, width)], users.at[b], users_sem.at[b])

    for copy in loads:
        copy.start()

    @pl.loop(0, 2 * chips)
    def _(b):
        users_load(b).start()

    barrier = pltpu.get_barrier_semaphore()
    pl.semaphore_signal(barrier, inc=1, device_id=partner, device_id_type=MESH)
    for step in range(1, groups):
        pl.semaphore_signal(
            barrier, inc=1, device_id=((g + step) % groups, c), device_id_type=MESH)

    @pl.when(z > 0)
    def _():
        pl.semaphore_signal(barrier, inc=1, device_id=below, device_id_type=MESH)

    @pl.when(z < chips - 1)
    def _():
        pl.semaphore_signal(barrier, inc=1, device_id=above, device_id_type=MESH)

    pl.semaphore_wait(
        barrier, groups + jnp.where(z > 0, 1, 0) + jnp.where(z < chips - 1, 1, 0))

    for copy in loads:
        copy.wait()
    factor3[...] = left_form(factor[...])

    def give_copy(i):
        return pltpu.make_async_remote_copy(
            src_ref=give.at[i], dst_ref=take.at[i], send_sem=give_sem.at[i],
            recv_sem=take_sem.at[i], device_id=partner, device_id_type=MESH)

    def up(i, q):
        return pltpu.make_async_remote_copy(
            src_ref=own.at[i, q], dst_ref=from_low.at[i, q], send_sem=hop_sem.at[i, q],
            recv_sem=low_sem.at[i, q], device_id=above, device_id_type=MESH)

    def down(i, q):
        return pltpu.make_async_remote_copy(
            src_ref=own.at[i, q], dst_ref=from_high.at[i, q], send_sem=hop_sem.at[i, q],
            recv_sem=high_sem.at[i, q], device_id=below, device_id_type=MESH)

    def send_first(i, q):
        d = i % chips

        @pl.when(jnp.logical_and(z == 0, d > 0))
        def _():
            up(i, q).start()

        if chips > 1:
            @pl.when(jnp.logical_and(z == chips - 1, d < chips - 1))
            def _():
                down(i, q).start()

    def merge(b):
        i = block_of(b)
        give_copy(i).wait()
        own[i] = own[i] + take[i]
        send_first(i, 0)

    @pl.loop(0, 2 * chips)
    def _(b):
        users_load(b).wait()
        i = block_of(b)
        product = dot(factor3[...], right_form(users[b]))
        for q in range(pieces):
            columns = slice(q * LANES, (q + 1) * LANES)
            own[i, q] = product[:half, columns]
            give[i, q] = product[half:, columns]
        give_copy(i).start()

        @pl.when(b > 0)
        def _():
            merge(b - 1)

    merge(2 * chips - 1)
    for q in range(1, pieces):
        @pl.loop(0, 2 * chips)
        def _(b):
            send_first(block_of(b), q)

    for copy in later:
        copy.start()

    def effect(h):
        @pl.loop(0, rows // (2 * LANES))
        def _(n):
            columns = pl.multiple_of(n * 2 * LANES, 2 * LANES)
            source = pl.multiple_of(h * rows + columns, 2 * LANES)
            product = dot(diag3[...], right_form(coupling[:, pl.ds(source, 2 * LANES)]))
            high, low = halves(product)
            effect3[h, :, pl.ds(columns, 2 * LANES)] = high
            effect3[h, :, pl.ds(rows + columns, 2 * LANES)] = high
            effect3[h, :, pl.ds(2 * rows + columns, 2 * LANES)] = low

    def total_copy(side, q):
        start = pl.multiple_of(e * half, half)
        return pltpu.make_async_remote_copy(
            src_ref=spare.at[q], dst_ref=total.at[q, pl.ds(start, half)],
            send_sem=spare_sem.at[q], recv_sem=total_sem.at[q],
            device_id=partner, device_id_type=MESH)

    def reduce_piece(p):
        q = p // 2
        side = p % 2

        def relay_up():
            for s in range(chips - 1):
                i = side * chips + chips - 1 - s

                @pl.when(jnp.logical_and(z > 0, chips - 1 - s > z))
                def _():
                    up(i, q).wait_recv()
                    own[i, q] = own[i, q] + from_low[i, q]
                    up(i, q).start()

        @pl.when(2 * z < chips)
        def _():
            relay_up()

        for s in range(chips - 1):
            i = side * chips + s

            @pl.when(jnp.logical_and(z < chips - 1, s < z))
            def _():
                down(i, q).wait_recv()
                own[i, q] = own[i, q] + from_high[i, q]
                down(i, q).start()

        @pl.when(2 * z >= chips)
        def _():
            relay_up()

        mine = side * chips + z

        @pl.when(z > 0)
        def _():
            up(mine, q).wait_recv()
            own[mine, q] = own[mine, q] + from_low[mine, q]

        @pl.when(z < chips - 1)
        def _():
            down(mine, q).wait_recv()
            own[mine, q] = own[mine, q] + from_high[mine, q]

        @pl.when(side == e)
        def _():
            total[q, pl.ds(pl.multiple_of(e * half, half), half)] = own[mine, q]

        @pl.when(side != e)
        def _():
            spare[q] = own[mine, q]
            total_copy(side, q).start()

    def solved_copy(source, target, q):
        return pltpu.make_async_remote_copy(
            src_ref=solved.at[q], dst_ref=arrived.at[source, q],
            send_sem=solved_sem.at[target, q], recv_sem=arrived_sem.at[source, q],
            device_id=(target, c), device_id_type=MESH)

    def solve_piece(q):
        columns = pl.ds(pl.multiple_of(q * LANES, LANES), LANES)
        total_copy(e, q).wait_recv()
        solved[q] = dot(diag3[...], right_form(rhs[:, columns] - total[q]))
        for h in range(groups - 1):
            @pl.when(h < g)
            def _():
                solved_copy(h, 0, q).wait_recv()
                solved[q] = solved[q] - dot(effect3[h], right_form(arrived[h, q]))
        for target in range(1, groups):
            @pl.when(target > g)
            def _():
                solved_copy(g, target, q).start()
        out_ref[:, columns] = solved[q]

    count = 2 * pieces

    @pl.loop(0, count + groups - 1)
    def _(t):
        @pl.when(t < count)
        def _():
            reduce_piece(t)

        @pl.when(t == 0)
        def _():
            for copy in later:
                copy.wait()
            diag3[...] = left_form(diag[...])

        p = t - g

        @pl.when(jnp.logical_and(jnp.logical_and(p >= 0, p < count), (p + 2 * groups) % 2 == e))
        def _():
            solve_piece(p // 2)

        @pl.when(jnp.logical_and(t < groups - 1, t < g))
        def _():
            effect(t)

    @pl.loop(0, 2 * chips)
    def _(i):
        @pl.when(i % chips != z)
        def _():
            for q in range(pieces):
                pltpu.make_async_remote_copy(
                    src_ref=own.at[i, q], dst_ref=from_low.at[i, q], send_sem=hop_sem.at[i, q],
                    recv_sem=low_sem.at[i, q], device_id=partner, device_id_type=MESH
                ).wait_send()

    for q in range(pieces):
        total_copy(0, q).wait_send()
        for target in range(1, groups):
            @pl.when(target > g)
            def _():
                solved_copy(g, target, q).wait_send()


def by_kernel(right_side, solved_factor, solved_users, diag_inverse, coupling):
    groups = lax.axis_size("grp")
    chips = lax.axis_size("col") // 2
    rows, width = right_side.shape
    depth = solved_factor.shape[1]
    half = rows // 2
    pieces = width // LANES
    f32, bf16 = jnp.float32, jnp.bfloat16
    unit = (half, LANES)
    blocks = 2 * chips
    dma = pltpu.SemaphoreType.DMA
    scratch = [
        pltpu.VMEM((rows, width), f32),
        pltpu.VMEM((rows, depth), f32),
        pltpu.VMEM((blocks, depth, width), f32),
        pltpu.VMEM((rows, rows), f32),
        pltpu.VMEM(coupling.shape, f32),
        pltpu.VMEM((rows, 3 * depth), bf16),
        pltpu.VMEM((rows, 3 * rows), bf16),
        pltpu.VMEM((groups - 1, rows, 3 * rows), bf16),
        pltpu.VMEM((blocks, pieces) + unit, f32),
        pltpu.VMEM((blocks, pieces) + unit, f32),
        pltpu.VMEM((blocks, pieces) + unit, f32),
        pltpu.VMEM((blocks, pieces) + unit, f32),
        pltpu.VMEM((blocks, pieces) + unit, f32),
        pltpu.VMEM((pieces, rows, LANES), f32),
        pltpu.VMEM((pieces,) + unit, f32),
        pltpu.VMEM((pieces, rows, LANES), f32),
        pltpu.VMEM((groups - 1, pieces, rows, LANES), f32),
        dma((5,)), dma((blocks,)), dma((blocks,)), dma((blocks,)),
        dma((blocks, pieces)), dma((blocks, pieces)), dma((blocks, pieces)),
        dma((pieces,)), dma((pieces,)), dma((groups, pieces)), dma((groups, pieces)),
    ]
    return pl.pallas_call(
        functools.partial(kernel, groups, chips, pieces),
        out_shape=jax.ShapeDtypeStruct((rows, width), f32),
        in_specs=[pl.BlockSpec(memory_space=pl.ANY)] * 5,
        out_specs=pl.BlockSpec(memory_space=pltpu.VMEM),
        scratch_shapes=scratch,
        compiler_params=pltpu.CompilerParams(
            collective_id=0, has_side_effects=True, vmem_limit_bytes=60 << 20),
    )(right_side, solved_factor, solved_users, diag_inverse, coupling)


def on_device(right_side, *others):
    whole_tiles = right_side.shape[1] % LANES == 0 and lax.axis_size("col") % 2 == 0
    return (by_kernel if whole_tiles else by_collectives)(right_side, *others)


def solution(mesh):
    placed = (P("grp", "col"), P("grp", "col"), P("col", None), P("grp", None), P("grp", None))
    return jax.shard_map(
        on_device, mesh=mesh, in_specs=placed, out_specs=P("grp", "col"), check_vma=False
    )
```

```python
import functools

import jax
import jax.numpy as jnp
from jax import lax
from jax.experimental import pallas as pl
from jax.experimental.pallas import tpu as pltpu
from jax.sharding import PartitionSpec as P

highest = lax.Precision.HIGHEST
MESH = pl.DeviceIdType.MESH
LANES = 128


def broadcast(block, axis, source):
    block = jnp.where(lax.axis_index(axis) == source, block, jnp.zeros_like(block))
    return lax.psum(block, axis)


def apply_plain(matrix, vector):
    return jnp.dot(matrix, vector, precision=highest, preferred_element_type=jnp.float32)


def run_chain(residue, diag_inverse, coupling, apply_left):
    groups = lax.axis_size("grp")
    position = lax.axis_index("grp")
    block_rows = diag_inverse.shape[0]
    result = jnp.zeros_like(residue)
    for section_index in range(groups):
        candidate = apply_left(diag_inverse, residue)
        result = jnp.where(position == section_index, candidate, result)
        if section_index + 1 < groups:
            solved = broadcast(candidate, "grp", section_index)
            coupling_block = coupling[
                :, section_index * block_rows : (section_index + 1) * block_rows
            ]
            residue = jnp.where(
                position > section_index, residue - apply_left(coupling_block, solved), residue
            )
    return result


def by_collectives(right_side, solved_factor, solved_users, diag_inverse, coupling):
    partials = jnp.dot(
        solved_factor, solved_users, precision=highest, preferred_element_type=jnp.float32
    )
    shares = lax.psum_scatter(partials, "col", scatter_dimension=1, tiled=True)
    residue = right_side - shares
    return run_chain(residue, diag_inverse, coupling, apply_plain)


def halves(x):
    high = x.astype(jnp.bfloat16)
    return high, (x - high.astype(jnp.float32)).astype(jnp.bfloat16)


def left_form(x):
    high, low = halves(x)
    return jnp.concatenate([high, high, low], axis=1)


def right_form(x):
    high, low = halves(x)
    return jnp.concatenate([high, low, high], axis=0)


def dot(a, b):
    return jnp.dot(a, b, preferred_element_type=jnp.float32)


def swap(x):
    return pltpu.roll(x, LANES // 2, 1)


def first_lanes(shape):
    return lax.broadcasted_iota(jnp.int32, shape, 1) < LANES // 2


def pack(x):
    upper, lower = x[: x.shape[0] // 2], x[x.shape[0] // 2 :]
    return jnp.where(first_lanes(upper.shape), upper, swap(lower))


def unpack(x):
    return jnp.concatenate([x, swap(x)], axis=0)


def kernel(
    groups, chips, pieces,
    rhs_hbm, factor_hbm, users_hbm, diag_hbm, coupling_hbm,
    out_ref,
    rhs, factor, users, diag, coupling,
    factor3, diag3, effect3,
    own, give, take, from_low, from_high, total, spare, work, solved, arrived,
    load_sem, users_sem, give_sem, take_sem, hop_sem, low_sem, high_sem,
    spare_sem, total_sem, solved_sem, arrived_sem,
):
    g = lax.axis_index("grp")
    c = lax.axis_index("col")
    z = c // 2
    e = c % 2
    rows = rhs.shape[0]
    half = rows // 2
    width = rhs.shape[1]
    partner = (g, z * 2 + (1 - e))
    above = (g, c + 2)
    below = (g, c - 2)

    def block_of(b):
        j = b % chips
        return (b // chips) * chips + jnp.where(2 * z < chips, chips - 1 - j, j)

    loads = []
    for part in range(2):
        source = pl.multiple_of((e if part == 0 else 1 - e) * half, half)
        loads.append(pltpu.make_async_copy(
            factor_hbm.at[pl.ds(source, half)], factor.at[pl.ds(part * half, half)],
            load_sem.at[part]))
    later = [
        pltpu.make_async_copy(diag_hbm, diag, load_sem.at[2]),
        pltpu.make_async_copy(coupling_hbm, coupling, load_sem.at[3]),
        pltpu.make_async_copy(rhs_hbm, rhs, load_sem.at[4]),
    ]

    def users_load(b):
        i = block_of(b)
        column = pl.multiple_of(((i % chips) * 2 + i // chips) * width, width)
        return pltpu.make_async_copy(
            users_hbm.at[:, pl.ds(column, width)], users.at[b], users_sem.at[b])

    for copy in loads:
        copy.start()

    @pl.loop(0, 2 * chips)
    def _(b):
        users_load(b).start()

    barrier = pltpu.get_barrier_semaphore()
    pl.semaphore_signal(barrier, inc=1, device_id=partner, device_id_type=MESH)
    for step in range(1, groups):
        pl.semaphore_signal(
            barrier, inc=1, device_id=((g + step) % groups, c), device_id_type=MESH)

    @pl.when(z > 0)
    def _():
        pl.semaphore_signal(barrier, inc=1, device_id=below, device_id_type=MESH)

    @pl.when(z < chips - 1)
    def _():
        pl.semaphore_signal(barrier, inc=1, device_id=above, device_id_type=MESH)

    for copy in loads:
        copy.wait()
    factor3[...] = left_form(factor[...])

    pl.semaphore_wait(
        barrier, groups + jnp.where(z > 0, 1, 0) + jnp.where(z < chips - 1, 1, 0))

    def give_copy(i):
        return pltpu.make_async_remote_copy(
            src_ref=give.at[i], dst_ref=take.at[i], send_sem=give_sem.at[i],
            recv_sem=take_sem.at[i], device_id=partner, device_id_type=MESH)

    def up(i, q):
        return pltpu.make_async_remote_copy(
            src_ref=own.at[i, q], dst_ref=from_low.at[i, q], send_sem=hop_sem.at[i, q],
            recv_sem=low_sem.at[i, q], device_id=above, device_id_type=MESH)

    def down(i, q):
        return pltpu.make_async_remote_copy(
            src_ref=own.at[i, q], dst_ref=from_high.at[i, q], send_sem=hop_sem.at[i, q],
            recv_sem=high_sem.at[i, q], device_id=below, device_id_type=MESH)

    def send_first(i, q):
        d = i % chips

        @pl.when(jnp.logical_and(z == 0, d > 0))
        def _():
            up(i, q).start()

        if chips > 1:
            @pl.when(jnp.logical_and(z == chips - 1, d < chips - 1))
            def _():
                down(i, q).start()

    def merge(b):
        i = block_of(b)
        give_copy(i).wait()
        own[i] = own[i] + take[i]
        send_first(i, 0)

    @pl.loop(0, 2 * chips)
    def _(b):
        users_load(b).wait()
        i = block_of(b)
        product = dot(factor3[...], right_form(users[b]))
        for q in range(pieces):
            columns = slice(q * LANES, (q + 1) * LANES)
            own[i, q] = product[:half, columns]
            give[i, q] = product[half:, columns]
        give_copy(i).start()

        @pl.when(b > 0)
        def _():
            merge(b - 1)

    merge(2 * chips - 1)
    for q in range(1, pieces):
        @pl.loop(0, 2 * chips)
        def _(b):
            send_first(block_of(b), q)

    for copy in later:
        copy.start()

    def effect(h):
        @pl.loop(0, rows // (2 * LANES))
        def _(n):
            columns = pl.multiple_of(n * 2 * LANES, 2 * LANES)
            source = pl.multiple_of(h * rows + columns, 2 * LANES)
            product = dot(diag3[...], right_form(coupling[:, pl.ds(source, 2 * LANES)]))
            high, low = halves(product)
            effect3[h, :, pl.ds(columns, 2 * LANES)] = high
            effect3[h, :, pl.ds(rows + columns, 2 * LANES)] = high
            effect3[h, :, pl.ds(2 * rows + columns, 2 * LANES)] = low

    def total_copy(side, q):
        start = pl.multiple_of(e * half, half)
        return pltpu.make_async_remote_copy(
            src_ref=spare.at[q], dst_ref=total.at[q, pl.ds(start, half)],
            send_sem=spare_sem.at[q], recv_sem=total_sem.at[q],
            device_id=partner, device_id_type=MESH)

    def reduce_piece(p):
        q = p // 2
        side = p % 2

        def relay_up():
            for s in range(chips - 1):
                i = side * chips + chips - 1 - s

                @pl.when(jnp.logical_and(z > 0, chips - 1 - s > z))
                def _():
                    up(i, q).wait_recv()
                    own[i, q] = own[i, q] + from_low[i, q]
                    up(i, q).start()

        @pl.when(2 * z < chips)
        def _():
            relay_up()

        for s in range(chips - 1):
            i = side * chips + s

            @pl.when(jnp.logical_and(z < chips - 1, s < z))
            def _():
                down(i, q).wait_recv()
                own[i, q] = own[i, q] + from_high[i, q]
                down(i, q).start()

        @pl.when(2 * z >= chips)
        def _():
            relay_up()

        mine = side * chips + z

        @pl.when(z > 0)
        def _():
            up(mine, q).wait_recv()
            own[mine, q] = own[mine, q] + from_low[mine, q]

        @pl.when(z < chips - 1)
        def _():
            down(mine, q).wait_recv()
            own[mine, q] = own[mine, q] + from_high[mine, q]

        @pl.when(side == e)
        def _():
            total[q, pl.ds(pl.multiple_of(e * half, half), half)] = own[mine, q]

        @pl.when(side != e)
        def _():
            spare[q] = own[mine, q]
            total_copy(side, q).start()

    def solved_copy(source, target, q, a):
        return pltpu.make_async_remote_copy(
            src_ref=solved.at[q, a], dst_ref=arrived.at[source, q, a],
            send_sem=solved_sem.at[target, q, a], recv_sem=arrived_sem.at[source, q, a],
            device_id=(target, c), device_id_type=MESH)

    last = jnp.maximum(g - 1, 0)

    def solve_piece(q):
        columns = pl.ds(pl.multiple_of(q * LANES, LANES), LANES)
        total_copy(e, q).wait_recv()
        work[...] = dot(diag3[...], right_form(rhs[:, columns] - total[q]))
        for h in range(groups - 2):
            @pl.when(h < g - 1)
            def _():
                solved_copy(h, 0, q, 0).wait_recv()
                solved_copy(h, 0, q, 1).wait_recv()
                first = unpack(arrived[h, q, 0])
                both = jnp.where(
                    first_lanes(first.shape), first, swap(unpack(arrived[h, q, 1])))
                work[...] = work[...] - dot(effect3[h], right_form(both))
        for a in range(2):
            @pl.when(g > 0)
            def _():
                solved_copy(last, 0, q, a).wait_recv()
                product = dot(effect3[last], right_form(unpack(arrived[last, q, a])))
                if a == 0:
                    mine = first_lanes(product.shape)
                else:
                    product = swap(product)
                    mine = jnp.logical_not(first_lanes(product.shape))
                work[...] = jnp.where(mine, work[...] - product, work[...])

            @pl.when(g < groups - 1)
            def _():
                solved[q, a] = pack(work[...] if a == 0 else swap(work[...]))
                solved_copy(g, g + 1, q, a).start()
        for target in range(2, groups):
            @pl.when(target > g + 1)
            def _():
                for a in range(2):
                    solved_copy(g, target, q, a).start()
        out_ref[:, columns] = work[...]

    count = 2 * pieces

    @pl.loop(0, count + groups - 1)
    def _(t):
        @pl.when(t < count)
        def _():
            reduce_piece(t)

        @pl.when(t == 0)
        def _():
            for copy in later:
                copy.wait()
            diag3[...] = left_form(diag[...])

        p = t - g

        @pl.when(jnp.logical_and(jnp.logical_and(p >= 0, p < count), (p + 2 * groups) % 2 == e))
        def _():
            solve_piece(p // 2)

        @pl.when(jnp.logical_and(t < groups - 1, t < g))
        def _():
            effect(t)

    @pl.loop(0, 2 * chips)
    def _(i):
        @pl.when(i % chips != z)
        def _():
            for q in range(pieces):
                pltpu.make_async_remote_copy(
                    src_ref=own.at[i, q], dst_ref=from_low.at[i, q], send_sem=hop_sem.at[i, q],
                    recv_sem=low_sem.at[i, q], device_id=partner, device_id_type=MESH
                ).wait_send()

    for q in range(pieces):
        total_copy(0, q).wait_send()
        for target in range(1, groups):
            @pl.when(target > g)
            def _():
                for a in range(2):
                    solved_copy(g, target, q, a).wait_send()


def by_kernel(right_side, solved_factor, solved_users, diag_inverse, coupling):
    groups = lax.axis_size("grp")
    chips = lax.axis_size("col") // 2
    rows, width = right_side.shape
    depth = solved_factor.shape[1]
    half = rows // 2
    pieces = width // LANES
    f32, bf16 = jnp.float32, jnp.bfloat16
    unit = (half, LANES)
    blocks = 2 * chips
    dma = pltpu.SemaphoreType.DMA
    scratch = [
        pltpu.VMEM((rows, width), f32),
        pltpu.VMEM((rows, depth), f32),
        pltpu.VMEM((blocks, depth, width), f32),
        pltpu.VMEM((rows, rows), f32),
        pltpu.VMEM(coupling.shape, f32),
        pltpu.VMEM((rows, 3 * depth), bf16),
        pltpu.VMEM((rows, 3 * rows), bf16),
        pltpu.VMEM((groups - 1, rows, 3 * rows), bf16),
        pltpu.VMEM((blocks, pieces) + unit, f32),
        pltpu.VMEM((blocks, pieces) + unit, f32),
        pltpu.VMEM((blocks, pieces) + unit, f32),
        pltpu.VMEM((blocks, pieces) + unit, f32),
        pltpu.VMEM((blocks, pieces) + unit, f32),
        pltpu.VMEM((pieces, rows, LANES), f32),
        pltpu.VMEM((pieces,) + unit, f32),
        pltpu.VMEM((rows, LANES), f32),
        pltpu.VMEM((pieces, 2) + unit, f32),
        pltpu.VMEM((groups - 1, pieces, 2) + unit, f32),
        dma((5,)), dma((blocks,)), dma((blocks,)), dma((blocks,)),
        dma((blocks, pieces)), dma((blocks, pieces)), dma((blocks, pieces)),
        dma((pieces,)), dma((pieces,)), dma((groups, pieces, 2)), dma((groups, pieces, 2)),
    ]
    return pl.pallas_call(
        functools.partial(kernel, groups, chips, pieces),
        out_shape=jax.ShapeDtypeStruct((rows, width), f32),
        in_specs=[pl.BlockSpec(memory_space=pl.ANY)] * 5,
        out_specs=pl.BlockSpec(memory_space=pltpu.VMEM),
        scratch_shapes=scratch,
        compiler_params=pltpu.CompilerParams(
            collective_id=0, has_side_effects=True, vmem_limit_bytes=60 << 20),
    )(right_side, solved_factor, solved_users, diag_inverse, coupling)


def on_device(right_side, *others):
    whole_tiles = right_side.shape[1] % LANES == 0 and lax.axis_size("col") % 2 == 0
    return (by_kernel if whole_tiles else by_collectives)(right_side, *others)


def solution(mesh):
    placed = (P("grp", "col"), P("grp", "col"), P("col", None), P("grp", None), P("grp", None))
    return jax.shard_map(
        on_device, mesh=mesh, in_specs=placed, out_specs=P("grp", "col"), check_vma=False
    )
```

```python
import functools

import jax
import jax.numpy as jnp
from jax import lax
from jax.experimental import pallas as pl
from jax.experimental.pallas import tpu as pltpu
from jax.sharding import PartitionSpec as P

highest = lax.Precision.HIGHEST
MESH = pl.DeviceIdType.MESH
LANES = 128


def broadcast(block, axis, source):
    block = jnp.where(lax.axis_index(axis) == source, block, jnp.zeros_like(block))
    return lax.psum(block, axis)


def apply_plain(matrix, vector):
    return jnp.dot(matrix, vector, precision=highest, preferred_element_type=jnp.float32)


def run_chain(residue, diag_inverse, coupling, apply_left):
    groups = lax.axis_size("grp")
    position = lax.axis_index("grp")
    block_rows = diag_inverse.shape[0]
    result = jnp.zeros_like(residue)
    for section_index in range(groups):
        candidate = apply_left(diag_inverse, residue)
        result = jnp.where(position == section_index, candidate, result)
        if section_index + 1 < groups:
            solved = broadcast(candidate, "grp", section_index)
            coupling_block = coupling[
                :, section_index * block_rows : (section_index + 1) * block_rows
            ]
            residue = jnp.where(
                position > section_index, residue - apply_left(coupling_block, solved), residue
            )
    return result


def by_collectives(right_side, solved_factor, solved_users, diag_inverse, coupling):
    partials = jnp.dot(
        solved_factor, solved_users, precision=highest, preferred_element_type=jnp.float32
    )
    shares = lax.psum_scatter(partials, "col", scatter_dimension=1, tiled=True)
    residue = right_side - shares
    return run_chain(residue, diag_inverse, coupling, apply_plain)


def halves(x):
    high = x.astype(jnp.bfloat16)
    return high, (x - high.astype(jnp.float32)).astype(jnp.bfloat16)


def left_form(x):
    high, low = halves(x)
    return jnp.concatenate([high, high, low], axis=1)


def right_form(x):
    high, low = halves(x)
    return jnp.concatenate([high, low, high], axis=0)


def dot(a, b):
    return jnp.dot(a, b, preferred_element_type=jnp.float32)


def swap(x):
    return pltpu.roll(x, LANES // 2, 1)


def first_lanes(shape):
    return lax.broadcasted_iota(jnp.int32, shape, 1) < LANES // 2


def pack(x):
    upper, lower = x[: x.shape[0] // 2], x[x.shape[0] // 2 :]
    return jnp.where(first_lanes(upper.shape), upper, swap(lower))


def unpack(x):
    return jnp.concatenate([x, swap(x)], axis=0)


def kernel(
    groups, chips, pieces,
    rhs_hbm, factor_hbm, users_hbm, diag_hbm, coupling_hbm,
    out_ref,
    rhs, factor, users, diag, coupling,
    factor3, diag3, effect3,
    own, give, take, from_low, from_high, total, spare, work, solved, arrived,
    load_sem, users_sem, give_sem, take_sem, hop_sem, low_sem, high_sem,
    spare_sem, total_sem, solved_sem, arrived_sem,
):
    g = lax.axis_index("grp")
    c = lax.axis_index("col")
    z = c // 2
    e = c % 2
    rows = rhs.shape[0]
    half = rows // 2
    width = rhs.shape[1]
    partner = (g, z * 2 + (1 - e))
    above = (g, c + 2)
    below = (g, c - 2)

    def block_of(b):
        j = b % chips
        return (b // chips) * chips + jnp.where(2 * z < chips, chips - 1 - j, j)

    loads = []
    for part in range(2):
        source = pl.multiple_of((e if part == 0 else 1 - e) * half, half)
        loads.append(pltpu.make_async_copy(
            factor_hbm.at[pl.ds(source, half)], factor.at[pl.ds(part * half, half)],
            load_sem.at[part]))
    later = [
        pltpu.make_async_copy(diag_hbm, diag, load_sem.at[2]),
        pltpu.make_async_copy(coupling_hbm, coupling, load_sem.at[3]),
        pltpu.make_async_copy(rhs_hbm, rhs, load_sem.at[4]),
    ]

    def users_load(b):
        i = block_of(b)
        column = pl.multiple_of(((i % chips) * 2 + i // chips) * width, width)
        return pltpu.make_async_copy(
            users_hbm.at[:, pl.ds(column, width)], users.at[b], users_sem.at[b])

    for copy in loads:
        copy.start()

    @pl.loop(0, 2 * chips)
    def _(b):
        users_load(b).start()

    barrier = pltpu.get_barrier_semaphore()
    pl.semaphore_signal(barrier, inc=1, device_id=partner, device_id_type=MESH)
    for step in range(1, groups):
        pl.semaphore_signal(
            barrier, inc=1, device_id=((g + step) % groups, c), device_id_type=MESH)

    @pl.when(z > 0)
    def _():
        pl.semaphore_signal(barrier, inc=1, device_id=below, device_id_type=MESH)

    @pl.when(z < chips - 1)
    def _():
        pl.semaphore_signal(barrier, inc=1, device_id=above, device_id_type=MESH)

    for copy in loads:
        copy.wait()
    factor3[...] = left_form(factor[...])

    pl.semaphore_wait(
        barrier, groups + jnp.where(z > 0, 1, 0) + jnp.where(z < chips - 1, 1, 0))

    def give_copy(i):
        return pltpu.make_async_remote_copy(
            src_ref=give.at[i], dst_ref=take.at[i], send_sem=give_sem.at[i],
            recv_sem=take_sem.at[i], device_id=partner, device_id_type=MESH)

    def up(i, q):
        return pltpu.make_async_remote_copy(
            src_ref=own.at[i, q], dst_ref=from_low.at[i, q], send_sem=hop_sem.at[i, q],
            recv_sem=low_sem.at[i, q], device_id=above, device_id_type=MESH)

    def down(i, q):
        return pltpu.make_async_remote_copy(
            src_ref=own.at[i, q], dst_ref=from_high.at[i, q], send_sem=hop_sem.at[i, q],
            recv_sem=high_sem.at[i, q], device_id=below, device_id_type=MESH)

    def send_first(i, q):
        d = i % chips

        @pl.when(jnp.logical_and(z == 0, d > 0))
        def _():
            up(i, q).start()

        if chips > 1:
            @pl.when(jnp.logical_and(z == chips - 1, d < chips - 1))
            def _():
                down(i, q).start()

    def merge(b):
        i = block_of(b)
        give_copy(i).wait()
        own[i] = own[i] + take[i]
        send_first(i, 0)

    @pl.loop(0, 2 * chips)
    def _(b):
        users_load(b).wait()
        i = block_of(b)
        product = dot(factor3[...], right_form(users[b]))
        for q in range(pieces):
            columns = slice(q * LANES, (q + 1) * LANES)
            own[i, q] = product[:half, columns]
            give[i, q] = product[half:, columns]
        give_copy(i).start()

        @pl.when(b > 0)
        def _():
            merge(b - 1)

    merge(2 * chips - 1)
    for q in range(1, pieces):
        @pl.loop(0, 2 * chips)
        def _(b):
            send_first(block_of(b), q)

    for copy in later:
        copy.start()

    def effect(h):
        @pl.loop(0, rows // (2 * LANES))
        def _(n):
            columns = pl.multiple_of(n * 2 * LANES, 2 * LANES)
            source = pl.multiple_of(h * rows + columns, 2 * LANES)
            product = dot(diag3[...], right_form(coupling[:, pl.ds(source, 2 * LANES)]))
            high, low = halves(product)
            effect3[h, :, pl.ds(columns, 2 * LANES)] = high
            effect3[h, :, pl.ds(rows + columns, 2 * LANES)] = high
            effect3[h, :, pl.ds(2 * rows + columns, 2 * LANES)] = low

    def total_copy(side, q):
        start = pl.multiple_of(e * half, half)
        return pltpu.make_async_remote_copy(
            src_ref=spare.at[q], dst_ref=total.at[q, pl.ds(start, half)],
            send_sem=spare_sem.at[q], recv_sem=total_sem.at[q],
            device_id=partner, device_id_type=MESH)

    def reduce_piece(p):
        q = p // 2
        side = p % 2

        def relay_up():
            for s in range(chips - 1):
                i = side * chips + chips - 1 - s

                @pl.when(jnp.logical_and(z > 0, chips - 1 - s > z))
                def _():
                    up(i, q).wait_recv()
                    own[i, q] = own[i, q] + from_low[i, q]
                    up(i, q).start()

        @pl.when(2 * z < chips)
        def _():
            relay_up()

        for s in range(chips - 1):
            i = side * chips + s

            @pl.when(jnp.logical_and(z < chips - 1, s < z))
            def _():
                down(i, q).wait_recv()
                own[i, q] = own[i, q] + from_high[i, q]
                down(i, q).start()

        @pl.when(2 * z >= chips)
        def _():
            relay_up()

        mine = side * chips + z

        @pl.when(z > 0)
        def _():
            up(mine, q).wait_recv()
            own[mine, q] = own[mine, q] + from_low[mine, q]

        @pl.when(z < chips - 1)
        def _():
            down(mine, q).wait_recv()
            own[mine, q] = own[mine, q] + from_high[mine, q]

        @pl.when(side == e)
        def _():
            total[q, pl.ds(pl.multiple_of(e * half, half), half)] = own[mine, q]

        @pl.when(side != e)
        def _():
            spare[q] = own[mine, q]
            total_copy(side, q).start()

    def solved_copy(source, target, q, a):
        return pltpu.make_async_remote_copy(
            src_ref=solved.at[q, a], dst_ref=arrived.at[source, q, a],
            send_sem=solved_sem.at[target, q, a], recv_sem=arrived_sem.at[source, q, a],
            device_id=(target, c), device_id_type=MESH)

    last = jnp.maximum(g - 1, 0)

    def solve_piece(q):
        columns = pl.ds(pl.multiple_of(q * LANES, LANES), LANES)
        total_copy(e, q).wait_recv()
        work[...] = dot(diag3[...], right_form(rhs[:, columns] - total[q]))
        for h in range(groups - 2):
            @pl.when(h < g - 1)
            def _():
                solved_copy(h, 0, q, 0).wait_recv()
                solved_copy(h, 0, q, 1).wait_recv()
                first = unpack(arrived[h, q, 0])
                both = jnp.where(
                    first_lanes(first.shape), first, swap(unpack(arrived[h, q, 1])))
                work[...] = work[...] - dot(effect3[h], right_form(both))
        for a in range(2):
            @pl.when(g > 0)
            def _():
                solved_copy(last, 0, q, a).wait_recv()
                product = dot(effect3[last], right_form(unpack(arrived[last, q, a])))
                if a == 0:
                    mine = first_lanes(product.shape)
                else:
                    product = swap(product)
                    mine = jnp.logical_not(first_lanes(product.shape))
                work[...] = jnp.where(mine, work[...] - product, work[...])

            @pl.when(g < groups - 1)
            def _():
                solved[q, a] = pack(work[...] if a == 0 else swap(work[...]))
                solved_copy(g, g + 1, q, a).start()
        for target in range(2, groups):
            @pl.when(target > g + 1)
            def _():
                for a in range(2):
                    solved_copy(g, target, q, a).start()
        out_ref[:, columns] = work[...]

    count = 2 * pieces

    @pl.loop(0, count + groups - 1)
    def _(t):
        @pl.when(t < count)
        def _():
            reduce_piece(t)

        @pl.when(t == 0)
        def _():
            for copy in later:
                copy.wait()
            diag3[...] = left_form(diag[...])

        p = t - g

        @pl.when(jnp.logical_and(jnp.logical_and(p >= 0, p < count), (p + 2 * groups) % 2 == e))
        def _():
            solve_piece(p // 2)

        @pl.when(jnp.logical_and(t < groups - 1, t < g))
        def _():
            effect(t)

    @pl.loop(0, 2 * chips)
    def _(i):
        @pl.when(i % chips != z)
        def _():
            for q in range(pieces):
                pltpu.make_async_remote_copy(
                    src_ref=own.at[i, q], dst_ref=from_low.at[i, q], send_sem=hop_sem.at[i, q],
                    recv_sem=low_sem.at[i, q], device_id=partner, device_id_type=MESH
                ).wait_send()

    for q in range(pieces):
        total_copy(0, q).wait_send()
        for target in range(1, groups):
            @pl.when(target > g)
            def _():
                for a in range(2):
                    solved_copy(g, target, q, a).wait_send()


def by_kernel(right_side, solved_factor, solved_users, diag_inverse, coupling):
    groups = lax.axis_size("grp")
    chips = lax.axis_size("col") // 2
    rows, width = right_side.shape
    depth = solved_factor.shape[1]
    half = rows // 2
    pieces = width // LANES
    f32, bf16 = jnp.float32, jnp.bfloat16
    unit = (half, LANES)
    blocks = 2 * chips
    dma = pltpu.SemaphoreType.DMA
    scratch = [
        pltpu.VMEM((rows, width), f32),
        pltpu.VMEM((rows, depth), f32),
        pltpu.VMEM((blocks, depth, width), f32),
        pltpu.VMEM((rows, rows), f32),
        pltpu.VMEM(coupling.shape, f32),
        pltpu.VMEM((rows, 3 * depth), bf16),
        pltpu.VMEM((rows, 3 * rows), bf16),
        pltpu.VMEM((groups - 1, rows, 3 * rows), bf16),
        pltpu.VMEM((blocks, pieces) + unit, f32),
        pltpu.VMEM((blocks, pieces) + unit, f32),
        pltpu.VMEM((blocks, pieces) + unit, f32),
        pltpu.VMEM((blocks, pieces) + unit, f32),
        pltpu.VMEM((blocks, pieces) + unit, f32),
        pltpu.VMEM((pieces, rows, LANES), f32),
        pltpu.VMEM((pieces,) + unit, f32),
        pltpu.VMEM((rows, LANES), f32),
        pltpu.VMEM((pieces, 2) + unit, f32),
        pltpu.VMEM((groups - 1, pieces, 2) + unit, f32),
        dma((5,)), dma((blocks,)), dma((blocks,)), dma((blocks,)),
        dma((blocks, pieces)), dma((blocks, pieces)), dma((blocks, pieces)),
        dma((pieces,)), dma((pieces,)), dma((groups, pieces, 2)), dma((groups, pieces, 2)),
    ]
    return pl.pallas_call(
        functools.partial(kernel, groups, chips, pieces),
        out_shape=pltpu.VMEM((rows, width), f32),
        in_specs=[pl.BlockSpec(memory_space=pl.ANY)] * 5,
        out_specs=pl.BlockSpec(memory_space=pltpu.VMEM),
        scratch_shapes=scratch,
        compiler_params=pltpu.CompilerParams(
            collective_id=0, has_side_effects=True, vmem_limit_bytes=63 << 20),
    )(right_side, solved_factor, solved_users, diag_inverse, coupling)


def on_device(right_side, *others):
    whole_tiles = right_side.shape[1] % LANES == 0 and lax.axis_size("col") % 2 == 0
    return (by_kernel if whole_tiles else by_collectives)(right_side, *others)


def solution(mesh):
    placed = (P("grp", "col"), P("grp", "col"), P("col", None), P("grp", None), P("grp", None))
    return jax.shard_map(
        on_device, mesh=mesh, in_specs=placed, out_specs=P("grp", "col"), check_vma=False
    )
```

```python
import functools

import jax
import jax.numpy as jnp
from jax import lax
from jax.experimental import pallas as pl
from jax.experimental.pallas import tpu as pltpu
from jax.sharding import PartitionSpec as P

highest = lax.Precision.HIGHEST
MESH = pl.DeviceIdType.MESH
LANES = 128


def broadcast(block, axis, source):
    block = jnp.where(lax.axis_index(axis) == source, block, jnp.zeros_like(block))
    return lax.psum(block, axis)


def apply_plain(matrix, vector):
    return jnp.dot(matrix, vector, precision=highest, preferred_element_type=jnp.float32)


def run_chain(residue, diag_inverse, coupling, apply_left):
    groups = lax.axis_size("grp")
    position = lax.axis_index("grp")
    block_rows = diag_inverse.shape[0]
    result = jnp.zeros_like(residue)
    for section_index in range(groups):
        candidate = apply_left(diag_inverse, residue)
        result = jnp.where(position == section_index, candidate, result)
        if section_index + 1 < groups:
            solved = broadcast(candidate, "grp", section_index)
            coupling_block = coupling[
                :, section_index * block_rows : (section_index + 1) * block_rows
            ]
            residue = jnp.where(
                position > section_index, residue - apply_left(coupling_block, solved), residue
            )
    return result


def by_collectives(right_side, solved_factor, solved_users, diag_inverse, coupling):
    partials = jnp.dot(
        solved_factor, solved_users, precision=highest, preferred_element_type=jnp.float32
    )
    shares = lax.psum_scatter(partials, "col", scatter_dimension=1, tiled=True)
    residue = right_side - shares
    return run_chain(residue, diag_inverse, coupling, apply_plain)


def halves(x):
    high = x.astype(jnp.bfloat16)
    return high, (x - high.astype(jnp.float32)).astype(jnp.bfloat16)


def left_form(x):
    high, low = halves(x)
    return jnp.concatenate([high, high, low], axis=1)


def right_form(x):
    high, low = halves(x)
    return jnp.concatenate([high, low, high], axis=0)


def dot(a, b):
    return jnp.dot(a, b, preferred_element_type=jnp.float32)


def swap(x):
    return pltpu.roll(x, LANES // 2, 1)


def first_lanes(shape):
    return lax.broadcasted_iota(jnp.int32, shape, 1) < LANES // 2


def pack(x):
    upper, lower = x[: x.shape[0] // 2], x[x.shape[0] // 2 :]
    return jnp.where(first_lanes(upper.shape), upper, swap(lower))


def unpack(x):
    return jnp.concatenate([x, swap(x)], axis=0)


def kernel(
    groups, chips, pieces,
    rhs_hbm, factor_hbm, users_hbm, diag_hbm, coupling_hbm,
    out_ref,
    rhs, factor, users, diag, coupling,
    factor3, diag3, effect3,
    own, give, take, from_low, from_high, total, spare, work, solved, arrived,
    load_sem, users_sem, give_sem, take_sem, hop_sem, low_sem, high_sem,
    spare_sem, total_sem, solved_sem, arrived_sem,
):
    g = lax.axis_index("grp")
    c = lax.axis_index("col")
    z = c // 2
    e = c % 2
    rows = rhs.shape[0]
    half = rows // 2
    width = rhs.shape[1]
    partner = (g, z * 2 + (1 - e))
    above = (g, c + 2)
    below = (g, c - 2)

    def block_of(b):
        j = b % chips
        return (b // chips) * chips + jnp.where(2 * z < chips, chips - 1 - j, j)

    loads = []
    for part in range(2):
        source = pl.multiple_of((e if part == 0 else 1 - e) * half, half)
        loads.append(pltpu.make_async_copy(
            factor_hbm.at[pl.ds(source, half)], factor.at[pl.ds(part * half, half)],
            load_sem.at[part]))
    later = [
        pltpu.make_async_copy(diag_hbm, diag, load_sem.at[2]),
        pltpu.make_async_copy(coupling_hbm, coupling, load_sem.at[3]),
        pltpu.make_async_copy(rhs_hbm, rhs, load_sem.at[4]),
    ]

    def users_load(b):
        i = block_of(b)
        column = pl.multiple_of(((i % chips) * 2 + i // chips) * width, width)
        return pltpu.make_async_copy(
            users_hbm.at[:, pl.ds(column, width)], users.at[b], users_sem.at[b])

    for copy in loads:
        copy.start()

    @pl.loop(0, 2 * chips)
    def _(b):
        users_load(b).start()

    out_ref[...] = jnp.zeros_like(out_ref)
    barrier = pltpu.get_barrier_semaphore()
    pl.semaphore_signal(barrier, inc=1, device_id=partner, device_id_type=MESH)
    for step in range(1, groups):
        pl.semaphore_signal(
            barrier, inc=1, device_id=((g + step) % groups, c), device_id_type=MESH)

    @pl.when(z > 0)
    def _():
        pl.semaphore_signal(barrier, inc=1, device_id=below, device_id_type=MESH)

    @pl.when(z < chips - 1)
    def _():
        pl.semaphore_signal(barrier, inc=1, device_id=above, device_id_type=MESH)

    for copy in loads:
        copy.wait()
    factor3[...] = left_form(factor[...])

    pl.semaphore_wait(
        barrier, groups + jnp.where(z > 0, 1, 0) + jnp.where(z < chips - 1, 1, 0))

    def give_copy(i):
        return pltpu.make_async_remote_copy(
            src_ref=give.at[i], dst_ref=take.at[i], send_sem=give_sem.at[i],
            recv_sem=take_sem.at[i], device_id=partner, device_id_type=MESH)

    def up(i, q):
        return pltpu.make_async_remote_copy(
            src_ref=own.at[i, q], dst_ref=from_low.at[i, q], send_sem=hop_sem.at[i, q],
            recv_sem=low_sem.at[i, q], device_id=above, device_id_type=MESH)

    def down(i, q):
        return pltpu.make_async_remote_copy(
            src_ref=own.at[i, q], dst_ref=from_high.at[i, q], send_sem=hop_sem.at[i, q],
            recv_sem=high_sem.at[i, q], device_id=below, device_id_type=MESH)

    def send_first(i, q):
        d = i % chips

        @pl.when(jnp.logical_and(z == 0, d > 0))
        def _():
            up(i, q).start()

        if chips > 1:
            @pl.when(jnp.logical_and(z == chips - 1, d < chips - 1))
            def _():
                down(i, q).start()

    def merge(b):
        i = block_of(b)
        give_copy(i).wait()
        own[i] = own[i] + take[i]
        send_first(i, 0)

    @pl.loop(0, 2 * chips)
    def _(b):
        users_load(b).wait()
        i = block_of(b)
        product = dot(factor3[...], right_form(users[b]))
        for k in range(pieces // 2):
            tile = product[:, k * LANES : (k + 1) * LANES]
            turned = swap(tile)
            own[i, 2 * k] = pack(tile[:half])
            own[i, 2 * k + 1] = pack(turned[:half])
            give[i, 2 * k] = pack(tile[half:])
            give[i, 2 * k + 1] = pack(turned[half:])
        give_copy(i).start()

        @pl.when(b > 0)
        def _():
            merge(b - 1)

    merge(2 * chips - 1)
    for q in range(1, pieces):
        @pl.loop(0, 2 * chips)
        def _(b):
            send_first(block_of(b), q)

    for copy in later:
        copy.start()

    def effect(h):
        @pl.loop(0, rows // (2 * LANES))
        def _(n):
            columns = pl.multiple_of(n * 2 * LANES, 2 * LANES)
            source = pl.multiple_of(h * rows + columns, 2 * LANES)
            product = dot(diag3[...], right_form(coupling[:, pl.ds(source, 2 * LANES)]))
            high, low = halves(product)
            effect3[h, :, pl.ds(columns, 2 * LANES)] = high
            effect3[h, :, pl.ds(rows + columns, 2 * LANES)] = high
            effect3[h, :, pl.ds(2 * rows + columns, 2 * LANES)] = low

    def total_copy(side, q):
        return pltpu.make_async_remote_copy(
            src_ref=spare.at[q], dst_ref=total.at[q, e],
            send_sem=spare_sem.at[q], recv_sem=total_sem.at[q],
            device_id=partner, device_id_type=MESH)

    def relay_up(q, side):
        for s in range(chips - 1):
            i = side * chips + chips - 1 - s

            @pl.when(jnp.logical_and(z > 0, chips - 1 - s > z))
            def _():
                up(i, q).wait_recv()
                own[i, q] = own[i, q] + from_low[i, q]
                up(i, q).start()

    def relay_down(q, side):
        for s in range(chips - 1):
            i = side * chips + s

            @pl.when(jnp.logical_and(z < chips - 1, s < z))
            def _():
                down(i, q).wait_recv()
                own[i, q] = own[i, q] + from_high[i, q]
                down(i, q).start()

    lower = 2 * z < chips

    def relay_near(p):
        @pl.when(lower)
        def _():
            relay_up(p // 2, p % 2)

        @pl.when(jnp.logical_not(lower))
        def _():
            relay_down(p // 2, p % 2)

    def finish_piece(p):
        q = p // 2
        side = p % 2

        @pl.when(lower)
        def _():
            relay_down(q, side)

        @pl.when(jnp.logical_not(lower))
        def _():
            relay_up(q, side)

        mine = side * chips + z

        @pl.when(z > 0)
        def _():
            up(mine, q).wait_recv()
            own[mine, q] = own[mine, q] + from_low[mine, q]

        @pl.when(z < chips - 1)
        def _():
            down(mine, q).wait_recv()
            own[mine, q] = own[mine, q] + from_high[mine, q]

        @pl.when(side == e)
        def _():
            total[q, e] = own[mine, q]

        @pl.when(side != e)
        def _():
            spare[q] = own[mine, q]
            total_copy(side, q).start()

    def solved_copy(source, target, q):
        return pltpu.make_async_remote_copy(
            src_ref=solved.at[q], dst_ref=arrived.at[source, q],
            send_sem=solved_sem.at[target, q], recv_sem=arrived_sem.at[source, q],
            device_id=(target, c), device_id_type=MESH)

    def solve_piece(q):
        columns = pl.ds(pl.multiple_of((q // 2) * LANES, LANES), LANES)
        odd = q % 2 == 1
        right = rhs[:, columns]
        right = jnp.where(odd, swap(right), right)
        total_copy(e, q).wait_recv()
        reduced = right - jnp.concatenate([unpack(total[q, 0]), unpack(total[q, 1])], axis=0)
        work[...] = dot(diag3[...], right_form(reduced))
        for h in range(groups - 1):
            @pl.when(h < g)
            def _():
                solved_copy(h, 0, q).wait_recv()
                work[...] = work[...] - dot(effect3[h], right_form(unpack(arrived[h, q])))
        result = work[...]

        @pl.when(g < groups - 1)
        def _():
            solved[q] = pack(result)
        for target in range(1, groups):
            @pl.when(target > g)
            def _():
                solved_copy(g, target, q).start()
        placed = jnp.where(odd, swap(result), result)
        mine = first_lanes(placed.shape) != odd
        out_ref[:, columns] = jnp.where(mine, placed, out_ref[:, columns])

    count = 2 * pieces

    relay_near(0)

    @pl.loop(0, count + groups - 1)
    def _(t):
        @pl.when(t + 1 < count)
        def _():
            relay_near(t + 1)

        @pl.when(t < count)
        def _():
            finish_piece(t)

        @pl.when(t == 0)
        def _():
            for copy in later:
                copy.wait()
            diag3[...] = left_form(diag[...])

        p = t - g

        @pl.when(jnp.logical_and(jnp.logical_and(p >= 0, p < count), (p + 2 * groups) % 2 == e))
        def _():
            solve_piece(p // 2)

        @pl.when(jnp.logical_and(t < groups - 1, t < g))
        def _():
            effect(t)

    @pl.loop(0, 2 * chips)
    def _(i):
        @pl.when(i % chips != z)
        def _():
            for q in range(pieces):
                pltpu.make_async_remote_copy(
                    src_ref=own.at[i, q], dst_ref=from_low.at[i, q], send_sem=hop_sem.at[i, q],
                    recv_sem=low_sem.at[i, q], device_id=partner, device_id_type=MESH
                ).wait_send()

    for q in range(pieces):
        total_copy(0, q).wait_send()
        for target in range(1, groups):
            @pl.when(target > g)
            def _():
                solved_copy(g, target, q).wait_send()


def by_kernel(right_side, solved_factor, solved_users, diag_inverse, coupling):
    groups = lax.axis_size("grp")
    chips = lax.axis_size("col") // 2
    rows, width = right_side.shape
    depth = solved_factor.shape[1]
    half = rows // 2
    pieces = width // (LANES // 2)
    f32, bf16 = jnp.float32, jnp.bfloat16
    unit = (half // 2, LANES)
    blocks = 2 * chips
    dma = pltpu.SemaphoreType.DMA
    scratch = [
        pltpu.VMEM((rows, width), f32),
        pltpu.VMEM((rows, depth), f32),
        pltpu.VMEM((blocks, depth, width), f32),
        pltpu.VMEM((rows, rows), f32),
        pltpu.VMEM(coupling.shape, f32),
        pltpu.VMEM((rows, 3 * depth), bf16),
        pltpu.VMEM((rows, 3 * rows), bf16),
        pltpu.VMEM((groups - 1, rows, 3 * rows), bf16),
        pltpu.VMEM((blocks, pieces) + unit, f32),
        pltpu.VMEM((blocks, pieces) + unit, f32),
        pltpu.VMEM((blocks, pieces) + unit, f32),
        pltpu.VMEM((blocks, pieces) + unit, f32),
        pltpu.VMEM((blocks, pieces) + unit, f32),
        pltpu.VMEM((pieces, 2) + unit, f32),
        pltpu.VMEM((pieces,) + unit, f32),
        pltpu.VMEM((rows, LANES), f32),
        pltpu.VMEM((pieces, half, LANES), f32),
        pltpu.VMEM((groups - 1, pieces, half, LANES), f32),
        dma((5,)), dma((blocks,)), dma((blocks,)), dma((blocks,)),
        dma((blocks, pieces)), dma((blocks, pieces)), dma((blocks, pieces)),
        dma((pieces,)), dma((pieces,)), dma((groups, pieces)), dma((groups, pieces)),
    ]
    return pl.pallas_call(
        functools.partial(kernel, groups, chips, pieces),
        out_shape=pltpu.VMEM((rows, width), f32),
        in_specs=[pl.BlockSpec(memory_space=pl.ANY)] * 5,
        out_specs=pl.BlockSpec(memory_space=pltpu.VMEM),
        scratch_shapes=scratch,
        compiler_params=pltpu.CompilerParams(
            collective_id=0, has_side_effects=True, vmem_limit_bytes=63 << 20),
    )(right_side, solved_factor, solved_users, diag_inverse, coupling)


def on_device(right_side, *others):
    whole_tiles = right_side.shape[1] % LANES == 0 and lax.axis_size("col") % 2 == 0
    return (by_kernel if whole_tiles else by_collectives)(right_side, *others)


def solution(mesh):
    placed = (P("grp", "col"), P("grp", "col"), P("col", None), P("grp", None), P("grp", None))
    return jax.shard_map(
        on_device, mesh=mesh, in_specs=placed, out_specs=P("grp", "col"), check_vma=False
    )
```

```python
import functools

import jax
import jax.numpy as jnp
from jax import lax
from jax.experimental import pallas as pl
from jax.experimental.pallas import tpu as pltpu
from jax.sharding import PartitionSpec as P

highest = lax.Precision.HIGHEST
MESH = pl.DeviceIdType.MESH
LANES = 128


def broadcast(block, axis, source):
    block = jnp.where(lax.axis_index(axis) == source, block, jnp.zeros_like(block))
    return lax.psum(block, axis)


def apply_plain(matrix, vector):
    return jnp.dot(matrix, vector, precision=highest, preferred_element_type=jnp.float32)


def run_chain(residue, diag_inverse, coupling, apply_left):
    groups = lax.axis_size("grp")
    position = lax.axis_index("grp")
    block_rows = diag_inverse.shape[0]
    result = jnp.zeros_like(residue)
    for section_index in range(groups):
        candidate = apply_left(diag_inverse, residue)
        result = jnp.where(position == section_index, candidate, result)
        if section_index + 1 < groups:
            solved = broadcast(candidate, "grp", section_index)
            coupling_block = coupling[
                :, section_index * block_rows : (section_index + 1) * block_rows
            ]
            residue = jnp.where(
                position > section_index, residue - apply_left(coupling_block, solved), residue
            )
    return result


def by_collectives(right_side, solved_factor, solved_users, diag_inverse, coupling):
    partials = jnp.dot(
        solved_factor, solved_users, precision=highest, preferred_element_type=jnp.float32
    )
    shares = lax.psum_scatter(partials, "col", scatter_dimension=1, tiled=True)
    residue = right_side - shares
    return run_chain(residue, diag_inverse, coupling, apply_plain)


def halves(x):
    high = x.astype(jnp.bfloat16)
    return high, (x - high.astype(jnp.float32)).astype(jnp.bfloat16)


def left_form(x):
    high, low = halves(x)
    return jnp.concatenate([high, high, low], axis=1)


def right_form(x):
    high, low = halves(x)
    return jnp.concatenate([high, low, high], axis=0)


def dot(a, b):
    return jnp.dot(a, b, preferred_element_type=jnp.float32)


def swap(x):
    return pltpu.roll(x, LANES // 2, 1)


def first_lanes(shape):
    return lax.broadcasted_iota(jnp.int32, shape, 1) < LANES // 2


def pack(x):
    upper, lower = x[: x.shape[0] // 2], x[x.shape[0] // 2 :]
    return jnp.where(first_lanes(upper.shape), upper, swap(lower))


def unpack(x):
    return jnp.concatenate([x, swap(x)], axis=0)


def kernel(
    groups, chips, pieces,
    rhs_hbm, factor_hbm, users_hbm, diag_hbm, coupling_hbm,
    out_ref,
    rhs, factor, users, diag, coupling,
    factor3, diag3, effect3,
    own, give, take, from_low, from_high, total, spare, work, solved, arrived,
    load_sem, users_sem, give_sem, take_sem, hop_sem, low_sem, high_sem,
    spare_sem, total_sem, solved_sem, arrived_sem,
):
    g = lax.axis_index("grp")
    c = lax.axis_index("col")
    z = c // 2
    e = c % 2
    rows = rhs.shape[0]
    half = rows // 2
    width = rhs.shape[1]
    partner = (g, z * 2 + (1 - e))
    above = (g, c + 2)
    below = (g, c - 2)

    def block_of(b):
        j = b % chips
        return (b // chips) * chips + jnp.where(2 * z < chips, chips - 1 - j, j)

    loads = []
    for part in range(2):
        source = pl.multiple_of((e if part == 0 else 1 - e) * half, half)
        loads.append(pltpu.make_async_copy(
            factor_hbm.at[pl.ds(source, half)], factor.at[pl.ds(part * half, half)],
            load_sem.at[part]))
    later = [
        pltpu.make_async_copy(diag_hbm, diag, load_sem.at[2]),
        pltpu.make_async_copy(coupling_hbm, coupling, load_sem.at[3]),
        pltpu.make_async_copy(rhs_hbm, rhs, load_sem.at[4]),
    ]

    def users_load(b):
        i = block_of(b)
        column = pl.multiple_of(((i % chips) * 2 + i // chips) * width, width)
        return pltpu.make_async_copy(
            users_hbm.at[:, pl.ds(column, width)], users.at[b], users_sem.at[b])

    for copy in loads:
        copy.start()

    @pl.loop(0, 2 * chips)
    def _(b):
        users_load(b).start()

    out_ref[...] = jnp.zeros_like(out_ref)
    barrier = pltpu.get_barrier_semaphore()
    pl.semaphore_signal(barrier, inc=1, device_id=partner, device_id_type=MESH)
    for step in range(1, groups):
        pl.semaphore_signal(
            barrier, inc=1, device_id=((g + step) % groups, c), device_id_type=MESH)

    @pl.when(z > 0)
    def _():
        pl.semaphore_signal(barrier, inc=1, device_id=below, device_id_type=MESH)

    @pl.when(z < chips - 1)
    def _():
        pl.semaphore_signal(barrier, inc=1, device_id=above, device_id_type=MESH)

    for copy in loads:
        copy.wait()
    factor3[...] = left_form(factor[...])

    pl.semaphore_wait(
        barrier, groups + jnp.where(z > 0, 1, 0) + jnp.where(z < chips - 1, 1, 0))

    def give_copy(i, q):
        return pltpu.make_async_remote_copy(
            src_ref=give.at[i, q], dst_ref=take.at[i, q], send_sem=give_sem.at[i, q],
            recv_sem=take_sem.at[i, q], device_id=partner, device_id_type=MESH)

    def up(i, q):
        return pltpu.make_async_remote_copy(
            src_ref=own.at[i, q], dst_ref=from_low.at[i, q], send_sem=hop_sem.at[i, q],
            recv_sem=low_sem.at[i, q], device_id=above, device_id_type=MESH)

    def down(i, q):
        return pltpu.make_async_remote_copy(
            src_ref=own.at[i, q], dst_ref=from_high.at[i, q], send_sem=hop_sem.at[i, q],
            recv_sem=high_sem.at[i, q], device_id=below, device_id_type=MESH)

    def send_first(i, q):
        d = i % chips

        @pl.when(jnp.logical_and(z == 0, d > 0))
        def _():
            up(i, q).start()

        if chips > 1:
            @pl.when(jnp.logical_and(z == chips - 1, d < chips - 1))
            def _():
                down(i, q).start()

    def merge(b):
        i = block_of(b)
        for q in range(pieces):
            give_copy(i, q).wait()
            own[i, q] = own[i, q] + take[i, q]
            if q == 0:
                send_first(i, 0)

    @pl.loop(0, 2 * chips)
    def _(b):
        users_load(b).wait()
        i = block_of(b)
        product = dot(factor3[...], right_form(users[b]))
        for k in range(pieces // 2):
            tile = product[:, k * LANES : (k + 1) * LANES]
            turned = swap(tile)
            own[i, 2 * k] = pack(tile[:half])
            own[i, 2 * k + 1] = pack(turned[:half])
            give[i, 2 * k] = pack(tile[half:])
            give[i, 2 * k + 1] = pack(turned[half:])
        for q in range(pieces):
            give_copy(i, q).start()

        @pl.when(b > 0)
        def _():
            merge(b - 1)

    merge(2 * chips - 1)
    for q in range(1, pieces):
        @pl.loop(0, 2 * chips)
        def _(b):
            send_first(block_of(b), q)

    for copy in later:
        copy.start()

    def effect(h):
        @pl.loop(0, rows // (2 * LANES))
        def _(n):
            columns = pl.multiple_of(n * 2 * LANES, 2 * LANES)
            source = pl.multiple_of(h * rows + columns, 2 * LANES)
            product = dot(diag3[...], right_form(coupling[:, pl.ds(source, 2 * LANES)]))
            high, low = halves(product)
            effect3[h, :, pl.ds(columns, 2 * LANES)] = high
            effect3[h, :, pl.ds(rows + columns, 2 * LANES)] = high
            effect3[h, :, pl.ds(2 * rows + columns, 2 * LANES)] = low

    def total_copy(side, q):
        return pltpu.make_async_remote_copy(
            src_ref=spare.at[q], dst_ref=total.at[q, e],
            send_sem=spare_sem.at[q], recv_sem=total_sem.at[q],
            device_id=partner, device_id_type=MESH)

    def relay_up(q, side):
        for s in range(chips - 1):
            i = side * chips + chips - 1 - s

            @pl.when(jnp.logical_and(z > 0, chips - 1 - s > z))
            def _():
                up(i, q).wait_recv()
                own[i, q] = own[i, q] + from_low[i, q]
                up(i, q).start()

    def relay_down(q, side):
        for s in range(chips - 1):
            i = side * chips + s

            @pl.when(jnp.logical_and(z < chips - 1, s < z))
            def _():
                down(i, q).wait_recv()
                own[i, q] = own[i, q] + from_high[i, q]
                down(i, q).start()

    lower = 2 * z < chips

    def relay_near(p):
        @pl.when(lower)
        def _():
            relay_up(p // 2, p % 2)

        @pl.when(jnp.logical_not(lower))
        def _():
            relay_down(p // 2, p % 2)

    def finish_piece(p):
        q = p // 2
        side = p % 2

        @pl.when(lower)
        def _():
            relay_down(q, side)

        @pl.when(jnp.logical_not(lower))
        def _():
            relay_up(q, side)

        mine = side * chips + z

        @pl.when(z > 0)
        def _():
            up(mine, q).wait_recv()
            own[mine, q] = own[mine, q] + from_low[mine, q]

        @pl.when(z < chips - 1)
        def _():
            down(mine, q).wait_recv()
            own[mine, q] = own[mine, q] + from_high[mine, q]

        @pl.when(side == e)
        def _():
            total[q, e] = own[mine, q]

        @pl.when(side != e)
        def _():
            spare[q] = own[mine, q]
            total_copy(side, q).start()

    def solved_copy(source, target, q):
        return pltpu.make_async_remote_copy(
            src_ref=solved.at[q], dst_ref=arrived.at[source, q],
            send_sem=solved_sem.at[target, q], recv_sem=arrived_sem.at[source, q],
            device_id=(target, c), device_id_type=MESH)

    def solve_piece(q):
        columns = pl.ds(pl.multiple_of((q // 2) * LANES, LANES), LANES)
        odd = q % 2 == 1
        right = rhs[:, columns]
        right = jnp.where(odd, swap(right), right)
        total_copy(e, q).wait_recv()
        reduced = right - jnp.concatenate([unpack(total[q, 0]), unpack(total[q, 1])], axis=0)
        work[...] = dot(diag3[...], right_form(reduced))
        for h in range(groups - 1):
            @pl.when(h < g)
            def _():
                solved_copy(h, 0, q).wait_recv()
                work[...] = work[...] - dot(effect3[h], right_form(unpack(arrived[h, q])))
        result = work[...]

        @pl.when(g < groups - 1)
        def _():
            solved[q] = pack(result)
        for target in range(1, groups):
            @pl.when(target > g)
            def _():
                solved_copy(g, target, q).start()
        placed = jnp.where(odd, swap(result), result)
        mine = first_lanes(placed.shape) != odd
        out_ref[:, columns] = jnp.where(mine, placed, out_ref[:, columns])

    count = 2 * pieces

    relay_near(0)

    @pl.loop(0, count + groups - 1)
    def _(t):
        @pl.when(t + 1 < count)
        def _():
            relay_near(t + 1)

        @pl.when(t < count)
        def _():
            finish_piece(t)

        @pl.when(t == 0)
        def _():
            for copy in later:
                copy.wait()
            diag3[...] = left_form(diag[...])

        p = t - g

        @pl.when(jnp.logical_and(jnp.logical_and(p >= 0, p < count), (p + 2 * groups) % 2 == e))
        def _():
            solve_piece(p // 2)

        @pl.when(jnp.logical_and(t < groups - 1, t < g))
        def _():
            effect(t)

    @pl.loop(0, 2 * chips)
    def _(i):
        @pl.when(i % chips != z)
        def _():
            for q in range(pieces):
                pltpu.make_async_remote_copy(
                    src_ref=own.at[i, q], dst_ref=from_low.at[i, q], send_sem=hop_sem.at[i, q],
                    recv_sem=low_sem.at[i, q], device_id=partner, device_id_type=MESH
                ).wait_send()

    for q in range(pieces):
        total_copy(0, q).wait_send()
        for target in range(1, groups):
            @pl.when(target > g)
            def _():
                solved_copy(g, target, q).wait_send()


def by_kernel(right_side, solved_factor, solved_users, diag_inverse, coupling):
    groups = lax.axis_size("grp")
    chips = lax.axis_size("col") // 2
    rows, width = right_side.shape
    depth = solved_factor.shape[1]
    half = rows // 2
    pieces = width // (LANES // 2)
    f32, bf16 = jnp.float32, jnp.bfloat16
    unit = (half // 2, LANES)
    blocks = 2 * chips
    dma = pltpu.SemaphoreType.DMA
    scratch = [
        pltpu.VMEM((rows, width), f32),
        pltpu.VMEM((rows, depth), f32),
        pltpu.VMEM((blocks, depth, width), f32),
        pltpu.VMEM((rows, rows), f32),
        pltpu.VMEM(coupling.shape, f32),
        pltpu.VMEM((rows, 3 * depth), bf16),
        pltpu.VMEM((rows, 3 * rows), bf16),
        pltpu.VMEM((groups - 1, rows, 3 * rows), bf16),
        pltpu.VMEM((blocks, pieces) + unit, f32),
        pltpu.VMEM((blocks, pieces) + unit, f32),
        pltpu.VMEM((blocks, pieces) + unit, f32),
        pltpu.VMEM((blocks, pieces) + unit, f32),
        pltpu.VMEM((blocks, pieces) + unit, f32),
        pltpu.VMEM((pieces, 2) + unit, f32),
        pltpu.VMEM((pieces,) + unit, f32),
        pltpu.VMEM((rows, LANES), f32),
        pltpu.VMEM((pieces, half, LANES), f32),
        pltpu.VMEM((groups - 1, pieces, half, LANES), f32),
        dma((5,)), dma((blocks,)), dma((blocks, pieces)), dma((blocks, pieces)),
        dma((blocks, pieces)), dma((blocks, pieces)), dma((blocks, pieces)),
        dma((pieces,)), dma((pieces,)), dma((groups, pieces)), dma((groups, pieces)),
    ]
    return pl.pallas_call(
        functools.partial(kernel, groups, chips, pieces),
        out_shape=pltpu.VMEM((rows, width), f32),
        in_specs=[pl.BlockSpec(memory_space=pl.ANY)] * 5,
        out_specs=pl.BlockSpec(memory_space=pltpu.VMEM),
        scratch_shapes=scratch,
        compiler_params=pltpu.CompilerParams(
            collective_id=0, has_side_effects=True, vmem_limit_bytes=63 << 20),
    )(right_side, solved_factor, solved_users, diag_inverse, coupling)


def on_device(right_side, *others):
    whole_tiles = right_side.shape[1] % LANES == 0 and lax.axis_size("col") % 2 == 0
    return (by_kernel if whole_tiles else by_collectives)(right_side, *others)


def solution(mesh):
    placed = (P("grp", "col"), P("grp", "col"), P("col", None), P("grp", None), P("grp", None))
    return jax.shard_map(
        on_device, mesh=mesh, in_specs=placed, out_specs=P("grp", "col"), check_vma=False
    )
```
